512 devices in a mesh: hour: 16 (over z), dom: 32 (over x, y, core).
Axes of the slice: x: 4, y: 4, z: 16, core: 2. Of those that a mesh axis runs over, the one named last changes fastest.
Arguments:
- query_matrix: bfloat16 [16, 4096, 1024], P('hour', 'dom'), may hold values from -1.6953125 to 1.6953125
- key_matrix: bfloat16 [16, 4096, 1024], P('hour', 'dom'), may hold values from -1.6953125 to 1.6953125
- value_matrix: bfloat16 [16, 4096, 1024], P('hour', 'dom'), may hold values from -6 to 6
- saved_output: bfloat16 [16, 4096, 1024], P('hour', 'dom'), may hold values from -6 to 6
- output_grad: bfloat16 [16, 4096, 1024], P('hour', 'dom'), may hold values from -16 to 16
- row_logsum: float32 [16, 16, 4096], P('hour', None, 'dom'), may hold values from 5.7 to 6.7
- key_blocks: int32 [32, 1], P('dom'), may hold values from 0 to 1, as said below
- halo_rows: int32 [32, 32, 4], replicated, may hold values from -1 to 127, as said below
Outputs:
- query_grad: bfloat16 [16, 4096, 1024], P('hour', 'dom')
- key_grad: bfloat16 [16, 4096, 1024], P('hour', 'dom')
- value_grad: bfloat16 [16, 4096, 1024], P('hour', 'dom')
The draws below stay inside these ranges and needn't reach their ends.
Inputs may be any that keep to these rules, and one draw needn't show every extreme that they name: `key_blocks`: row d + b holds 1 distinct candidate blocks in increasing order for query block b of partition d. `halo_rows`: entry [d, p, c] is the row, within partition p, that partition d receives in slot c, or -1 for an empty slot. No partition receives from itself; from each partition the live slots come first; partition d receives 4 live rows from partition (d + 1) % 32; entry c lies in rows c * (32) to (c + 1) * 32 - 1.
All inputs are finite; a program needn't handle non-finite values.
Results may differ from the reference program's by a relative error of at most 0.0049.
Values may be sent and summed in bfloat16 or wider, within the bound.
No kernel may reach another device: no remote copies, remote signals or barrier semaphores. Data moves between devices by JAX's collectives and lax.ppermute only.
A program may use at most 64 MiB of HBM per device.

```python
import jax
import jax.numpy as jnp
from jax import lax

HEADS = 16
HD = 64
D = 1024
BLK = 128
BLK_DEV = 1
TOK_DEV = 128
BUSES = 4096
HOURS = 16
HALO = 128
CAP = 4
CAND = 2
LK = 1
NQB = 32
N_DOM = 32


def draw_key_blocks(key, part):
    excluded = jax.random.randint(key, (NQB,), 0, CAND)
    excluded = excluded.at[0].set(0).at[1].set(CAND - 1)
    listed = jnp.arange(LK, dtype=jnp.int32)
    shifted = (listed[None, :] >= excluded[:, None]).astype(jnp.int32)
    return (listed[None, :] + shifted).astype(jnp.int32)


def draw_halo_rows(key, part):
    first_key, second_key, third_key = jax.random.split(key, 3)
    heavy = jax.random.randint(first_key, (N_DOM, N_DOM), 0, 4)
    light = jax.random.randint(second_key, (N_DOM, N_DOM), 0, CAP // 2 + 1)
    counts = jnp.where(heavy == 0, CAP, light)
    receiver = jnp.arange(N_DOM)[:, None]
    sender = jnp.arange(N_DOM)[None, :]
    counts = jnp.where(sender == (receiver + 1) % N_DOM, CAP, counts)
    counts = jnp.where(sender == receiver, 0, counts)
    stride = TOK_DEV // CAP
    offsets = jax.random.randint(third_key, (N_DOM, N_DOM, CAP), 0, stride)
    offsets = offsets.at[0, 1, CAP - 1].set(stride - 1)
    slots = jnp.arange(CAP)
    rows_drawn = slots[None, None, :] * stride + offsets
    return jnp.where(slots[None, None, :] < counts[:, :, None], rows_drawn, -1).astype(jnp.int32)


def shard_levels(key, shape, shards, low, top_value):
    factor_of, own = 1.0, jax.random.fold_in(key, 6)
    for axis_at, shards_of in shards:
        draws = jnp.exp(jax.random.uniform(jax.random.fold_in(own, axis_at), (shards_of,), jnp.float32, low / len(shards), top_value / len(shards)))
        factor_of = factor_of * jnp.repeat(draws, shape[axis_at] // shards_of).reshape([-1 if axis == axis_at else 1 for axis in range(len(shape))])
    return factor_of


def noise(key, dims, width, bound, shards=(), kind=jnp.bfloat16):
    gain = shard_levels(key, dims, shards, -0.22, 0.18) if shards else 1.0
    values = jax.random.normal(key, dims, jnp.float32) * width * gain
    return jnp.minimum(jnp.maximum(values, -bound), bound).astype(kind)


def setup_inputs(seed: int = 0) -> dict:
    streams_of = jax.random.split(jax.random.key(seed), 9)
    query_matrix = jnp.clip(jax.random.uniform(streams_of[0], (HOURS, BUSES, D), jnp.float32, -1.6953125, 1.6953125) * shard_levels(streams_of[0], (HOURS, BUSES, D), ((0, 16), (1, 32)), -0.4, 0.0), -1.6953125, 1.6953125).astype(jnp.bfloat16)
    key_matrix = jnp.clip(jax.random.uniform(streams_of[1], (HOURS, BUSES, D), jnp.float32, -1.6953125, 1.6953125) * shard_levels(streams_of[1], (HOURS, BUSES, D), ((0, 16), (1, 32)), -0.4, 0.0), -1.6953125, 1.6953125).astype(jnp.bfloat16)
    value_matrix = noise(streams_of[2], (HOURS, BUSES, D), 1.0, 6.0, ((0, 16), (1, 32)))
    saved_output = noise(streams_of[3], (HOURS, BUSES, D), 1.0, 6.0, ((0, 16), (1, 32)))
    output_grad = noise(streams_of[4], (HOURS, BUSES, D), 4.0, 16.0, ((0, 16), (1, 32)))
    row_logsum = jnp.clip(5.7 + 1.0 * jax.random.uniform(streams_of[5], (HOURS, HEADS, BUSES), jnp.float32) ** shard_levels(streams_of[5], (HOURS, HEADS, BUSES), ((0, 16), (2, 32)), -0.2, 0.2), 5.7, 6.7)
    key_blocks = draw_key_blocks(jax.random.fold_in(streams_of[8], 71), 0)
    halo_rows = draw_halo_rows(jax.random.fold_in(streams_of[8], 71), 0)
    return dict(query_matrix=query_matrix, key_matrix=key_matrix, value_matrix=value_matrix, saved_output=saved_output, output_grad=output_grad, row_logsum=row_logsum, key_blocks=key_blocks, halo_rows=halo_rows)


def widen(array):
    return array.astype(jnp.float32)


def rounded(array):
    return lax.optimization_barrier(array.astype(jnp.bfloat16)).astype(jnp.float32)


def attend(queries, cotangent, logsum, row_delta, key_set, value_set, live_mask):
    query_count = queries.shape[0]
    key_count = key_set.shape[0]
    factor = HD ** -0.5
    query_heads = widen(queries).reshape(query_count, HEADS, HD)
    cot_heads = widen(cotangent).reshape(query_count, HEADS, HD)
    key_heads = widen(key_set).reshape(key_count, HEADS, HD)
    value_heads = widen(value_set).reshape(key_count, HEADS, HD)
    scores = jnp.einsum("qhd,khd->hqk", query_heads, key_heads) * factor
    weights = jnp.where(live_mask[None, None, :], jnp.exp(scores - logsum[:, :, None]), 0.0)
    grad_weights = jnp.einsum("qhd,khd->hqk", cot_heads, value_heads)
    grad_scores = weights * (grad_weights - row_delta[:, :, None])
    weights_low = rounded(weights)
    grad_low = rounded(grad_scores)
    grad_values = jnp.einsum("hqk,qhd->khd", weights_low, cot_heads)
    grad_keys = jnp.einsum("hqk,qhd->khd", grad_low, query_heads) * factor
    grad_query = jnp.einsum("hqk,khd->qhd", grad_low, key_heads) * factor
    return grad_query.reshape(query_count, D), grad_keys.reshape(key_count, D), grad_values.reshape(key_count, D)


def reference(query_matrix, key_matrix, value_matrix, saved_output, output_grad, row_logsum, key_blocks, halo_rows):
    slots = jnp.arange(HALO, dtype=jnp.int32)
    owners = slots // CAP
    slot_row = halo_rows[:, owners, slots % CAP]
    halo_bus = owners[None, :] * TOK_DEV + jnp.maximum(slot_row, 0)
    local_bus = jnp.arange(N_DOM, dtype=jnp.int32)[:, None] * TOK_DEV + jnp.arange(TOK_DEV, dtype=jnp.int32)[None, :]
    pool_bus = jnp.concatenate([local_bus, halo_bus], axis=1).reshape(N_DOM, CAND, BLK)
    pool_live = jnp.concatenate([jnp.ones((N_DOM, TOK_DEV), jnp.bool_), slot_row >= 0], axis=1).reshape(N_DOM, CAND, BLK)
    zero_index = jnp.zeros((), jnp.int32)

    def visit(totals, position):
        grad_keys, grad_values = totals
        hour_id = (position // (N_DOM * BLK_DEV)).astype(jnp.int32)
        domain = ((position // BLK_DEV) % N_DOM).astype(jnp.int32)
        block_id = (position % BLK_DEV).astype(jnp.int32)
        chosen = key_blocks[domain * BLK_DEV + block_id]
        first_bus = (domain * TOK_DEV + block_id * BLK).astype(jnp.int32)
        own_bus = first_bus + jnp.arange(BLK, dtype=jnp.int32)
        cand_bus = pool_bus[domain][chosen].reshape(-1)
        cand_live = pool_live[domain][chosen].reshape(-1)
        bus_list = jnp.concatenate([cand_bus, own_bus, own_bus]).astype(jnp.int32)
        prev_hour = jnp.maximum(hour_id - 1, 0)
        next_hour = jnp.minimum(hour_id + 1, HOURS - 1)
        hour_list = jnp.concatenate([
            jnp.full((LK * BLK,), hour_id, jnp.int32),
            jnp.full((BLK,), prev_hour, jnp.int32),
            jnp.full((BLK,), next_hour, jnp.int32)]).astype(jnp.int32)
        live_list = jnp.concatenate([cand_live, jnp.full((BLK,), hour_id > 0), jnp.full((BLK,), hour_id < HOURS - 1)])
        queries = lax.dynamic_slice(query_matrix, (hour_id, first_bus, zero_index), (1, BLK, D))[0]
        cotangent = lax.dynamic_slice(output_grad, (hour_id, first_bus, zero_index), (1, BLK, D))[0]
        saved = lax.dynamic_slice(saved_output, (hour_id, first_bus, zero_index), (1, BLK, D))[0]
        logsum = lax.dynamic_slice(row_logsum, (hour_id, zero_index, first_bus), (1, HEADS, BLK))[0]
        products = widen(cotangent) * widen(saved)
        row_delta = jnp.sum(products.reshape(BLK, HEADS, HD), axis=2).T
        key_set = key_matrix[hour_list, bus_list]
        value_set = value_matrix[hour_list, bus_list]
        grad_query, grad_k, grad_v = attend(queries, cotangent, logsum, row_delta, key_set, value_set, live_list)
        grad_keys = grad_keys.at[hour_list, bus_list].add(grad_k)
        grad_values = grad_values.at[hour_list, bus_list].add(grad_v)
        return (grad_keys, grad_values), grad_query.astype(jnp.bfloat16)

    empty_grads = jnp.zeros((HOURS, BUSES, D), jnp.float32)
    positions = jnp.arange(HOURS * N_DOM * BLK_DEV, dtype=jnp.int32)
    (grad_keys, grad_values), query_blocks = lax.scan(visit, (empty_grads, empty_grads), positions)
    query_grad = query_blocks.reshape(HOURS, BUSES, D)
    return query_grad, grad_keys.astype(jnp.bfloat16), grad_values.astype(jnp.bfloat16)
```

```python
import functools
import math

import jax
import jax.numpy as jnp
from jax import lax
from jax.experimental import pallas as pl
from jax.experimental.pallas import tpu as pltpu
from jax.sharding import PartitionSpec as P

BF = jnp.bfloat16
F32 = jnp.float32
LANES = 128
VMEM_LIMIT = 24 << 20


def dot(a, b):
    return lax.dot_general(a, b, (((1,), (0,)), ((), ())), preferred_element_type=F32)


def dot_nt(a, b):
    return lax.dot_general(a, b, (((1,), (1,)), ((), ())), preferred_element_type=F32)


def dot_tn(a, b):
    return lax.dot_general(a, b, (((0,), (0,)), ((), ())), preferred_element_type=F32)


def iota(shape, dim):
    return lax.broadcasted_iota(jnp.int32, shape, dim)


def one_where(mask):
    return jnp.where(mask, 1.0, 0.0).astype(BF)


def split3(x):
    hi = x.astype(BF)
    rest = x - hi.astype(F32)
    mid = rest.astype(BF)
    return hi, mid, (rest - mid.astype(F32)).astype(BF)


def fetch(copies):
    for copy in copies:
        copy.start()
    return copies


def picks(halo, me, cap, slots, tokens, by_slot):
    rows = halo.astype(F32)
    twice = jnp.concatenate([rows, rows], axis=1)
    table = twice.reshape(slots, twice.shape[2]).astype(BF)
    owners = table.shape[1]
    shape = (slots, tokens) if by_slot else (tokens, slots)
    if by_slot:
        wanted = dot(table, one_where(iota((owners, tokens), 0) == me))
    else:
        wanted = dot_nt(one_where(iota((tokens, owners), 1) == me), table)
    slot_dim = 0 if by_slot else 1
    hit = wanted.astype(jnp.int32) == iota(shape, 1 - slot_dim)
    is_key = (iota(shape, slot_dim) % (2 * cap)) < cap
    both = [one_where(hit & is_key), one_where(hit & ~is_key)]
    return jnp.concatenate(both, axis=1 - slot_dim)


def front_kernel(
    me_ref,
    halo_hbm,
    query_hbm,
    key_hbm,
    value_hbm,
    cot_hbm,
    saved_hbm,
    logsum_hbm,
    pack_ref,
    send_hbm,
    halo_ref,
    saved_ref,
    logsum_ref,
    send_ref,
    sems,
):
    tokens, width = query_hbm.shape
    heads = logsum_hbm.shape[0]
    head_dim = width // heads
    slots = send_ref.shape[0]
    cap = halo_hbm.shape[1]
    pieces = [
        (halo_hbm, halo_ref),
        (key_hbm, pack_ref.at[:, width : 2 * width]),
        (value_hbm, pack_ref.at[:, 2 * width : 3 * width]),
        (cot_hbm, pack_ref.at[:, 3 * width : 4 * width]),
        (saved_hbm, saved_ref),
        (logsum_hbm, logsum_ref),
        (query_hbm, pack_ref.at[:, :width]),
    ]
    copies = fetch(
        [pltpu.make_async_copy(a, b, sems.at[i]) for i, (a, b) in enumerate(pieces)]
    )
    copies[0].wait()
    pick = picks(halo_ref[...], me_ref[0], cap, slots, tokens, True)
    copies[1].wait()
    copies[2].wait()
    both = jnp.concatenate(
        [pack_ref[:, width : 2 * width], pack_ref[:, 2 * width : 3 * width]], axis=0
    )
    send_ref[...] = dot(pick, both).astype(BF)
    out = pltpu.make_async_copy(send_ref, send_hbm, sems.at[len(pieces)])
    out.start()
    for copy in copies[3:]:
        copy.wait()
    product = pack_ref[:, 3 * width : 4 * width].astype(F32) * saved_ref[...].astype(F32)
    high = product.astype(BF)
    low = (product - high.astype(F32)).astype(BF)
    member = one_where(iota((heads, width), 1) // head_dim == iota((heads, width), 0))
    delta = dot_nt(member, high) + dot_nt(member, low)
    parts = [p.astype(F32) for p in split3(logsum_ref[...]) + split3(delta)]
    parts.append(jnp.zeros((LANES - 6 * heads, tokens), F32))
    pack_ref[:, 4 * width :] = jnp.concatenate(parts, axis=0).T.astype(BF)
    out.wait()


def extra_mask(head, heads, first):
    lane = iota((16, LANES), 1)
    inside = (lane >= first) & (lane < first + 3 * heads)
    return one_where(inside & (lane % heads == head))


def rows_of(pattern, tokens):
    return jnp.concatenate([pattern] * (tokens // pattern.shape[0]), axis=0)


def half_masks(tokens, head_dim):
    low = one_where(iota((16, LANES), 1) < head_dim)
    high = one_where(iota((16, LANES), 1) >= head_dim)
    return rows_of(low, tokens), rows_of(high, tokens)


def weights_of(rows, row_extra, columns, column_extra, scale):
    left = jnp.concatenate([rows, row_extra], axis=1)
    right = jnp.concatenate([columns, column_extra], axis=1)
    return dot_nt(left, right)


def key_side(keys, values, two_query, two_cot, two_logsum, two_delta, constants, scale):
    minus_inverse, minus_one = constants
    score = weights_of(keys, minus_inverse, two_query, two_logsum, scale)
    grad = weights_of(values, minus_one, two_cot, two_delta, scale)
    weight = jnp.exp2(score * (scale * math.log2(math.e)))
    grad_low = (weight * grad).astype(BF)
    value_grad = dot(weight.astype(BF), two_cot)
    key_grad = dot(grad_low, two_query)
    return key_grad, value_grad, grad_low


def two_heads(block, masks):
    return jnp.concatenate([block * masks[0], block * masks[1]], axis=0)


def two_extras(extra, pair, heads, first):
    tokens = extra.shape[0]
    return jnp.concatenate(
        [extra * rows_of(extra_mask(2 * pair + i, heads, first), tokens) for i in (0, 1)], axis=0
    )


def spread(slots, cap, by_slot):
    half = slots // 2
    shape = (slots, half) if by_slot else (half, slots)
    row, column = iota(shape, 0 if by_slot else 1), iota(shape, 1 if by_slot else 0)
    owner, place = row // (2 * cap), row % (2 * cap)
    keys = one_where((place < cap) & (column == owner * cap + place))
    values = one_where((place >= cap) & (column == owner * cap + place - cap))
    return jnp.concatenate([keys, values], axis=1 if by_slot else 0)


def halo_kernel(
    heads, cap, block_ref, pack_ref, recv_ref, part_hbm, back_hbm, pool, part, back, sems
):
    tokens = pack_ref.shape[0]
    slots, width = recv_ref.shape
    head_dim = width // heads
    scale = head_dim**-0.5
    local = block_ref[0] == 0

    @pl.when(local)
    def _():
        pool[:tokens] = pack_ref[:, width : 2 * width]
        pool[tokens:] = pack_ref[:, 2 * width : 3 * width]

    @pl.when(jnp.logical_not(local))
    def _():
        pool[...] = dot(spread(slots, cap, False), recv_ref[...]).astype(BF)

    masks = half_masks(tokens, head_dim)
    extra = pack_ref[:, 4 * width :]
    constants = (
        jnp.full((tokens, LANES), -1.0 / scale, BF),
        jnp.full((tokens, LANES), -1.0, BF),
    )
    low_lane = iota((tokens, LANES), 1) < head_dim
    layout = spread(slots, cap, True)
    to_own = jnp.where(local, 1.0, 0.0)
    to_halo = 1.0 - to_own
    outs = []
    for quad in range(heads // 4):
        both = []
        for pair in (2 * quad, 2 * quad + 1):
            at = pair * LANES
            keys = pool[:tokens, at : at + LANES]
            values = pool[tokens:, at : at + LANES]
            two_query = two_heads(pack_ref[:, at : at + LANES], masks)
            two_cot = two_heads(pack_ref[:, 3 * width + at : 3 * width + at + LANES], masks)
            key_grad, value_grad, grad_low = key_side(
                keys,
                values,
                two_query,
                two_cot,
                two_extras(extra, pair, heads, 0),
                two_extras(extra, pair, heads, 3 * heads),
                constants,
                scale,
            )
            key_grad = key_grad * scale
            query_grad = dot_tn(grad_low, keys)
            part[:tokens, at : at + LANES] = jnp.where(
                low_lane, query_grad[:tokens], query_grad[tokens:]
            )
            part[tokens : 2 * tokens, at : at + LANES] = key_grad * to_own
            part[2 * tokens :, at : at + LANES] = value_grad * to_own
            both.append(
                jnp.concatenate([key_grad * to_halo, value_grad * to_halo], axis=0).astype(BF)
            )
        lanes = slice(2 * quad * LANES, 2 * (quad + 1) * LANES)
        back[:, lanes] = dot(layout, jnp.concatenate(both, axis=1)).astype(BF)
        outs += fetch(
            [
                pltpu.make_async_copy(part.at[:, lanes], part_hbm.at[:, lanes], sems.at[2 * quad]),
                pltpu.make_async_copy(
                    back.at[:, lanes], back_hbm.at[:, lanes], sems.at[2 * quad + 1]
                ),
            ]
        )
    for copy in outs:
        copy.wait()


def hours_kernel(
    heads,
    me_ref,
    halo_hbm,
    pack_ref,
    first_hbm,
    second_hbm,
    part_hbm,
    query_hbm,
    total_ref,
    place_ref,
    halo_ref,
    first_ref,
    second_ref,
    part_ref,
    query_ref,
    sems,
):
    tokens, width = query_hbm.shape
    head_dim = width // heads
    scale = head_dim**-0.5
    pieces = [
        (halo_hbm, halo_ref),
        (part_hbm, part_ref),
        (first_hbm, first_ref),
        (second_hbm, second_ref),
    ]
    copies = fetch(
        [pltpu.make_async_copy(a, b, sems.at[i]) for i, (a, b) in enumerate(pieces)]
    )
    copies[0].wait()
    cap = halo_ref.shape[1]
    slots = place_ref.shape[1]
    place_ref[...] = picks(halo_ref[...], me_ref[0], cap, slots, tokens, False)
    for copy in copies[1:]:
        copy.wait()
    masks = half_masks(tokens, head_dim)
    own_extra = pack_ref[:, 4 * width :]
    constants = (
        jnp.full((tokens, LANES), -1.0 / scale, BF),
        jnp.full((tokens, LANES), -1.0, BF),
    )
    outs = []
    for pair in range(heads // 2):
        at = pair * LANES
        lanes = slice(at, at + LANES)
        own = [pack_ref[:, i * width + at : i * width + at + LANES] for i in range(4)]
        query_total = part_ref[:tokens, lanes]
        key_total = jnp.zeros((tokens, LANES), F32)
        value_total = part_ref[2 * tokens :, lanes]
        logsum_lanes, delta_lanes = (
            jnp.concatenate(
                [rows_of(extra_mask(2 * pair + i, heads, at_lane) * BF(by), tokens) for i in (0, 1)],
                axis=0,
            )
            for at_lane, by in ((0, -1.0 / scale), (3 * heads, -1.0))
        )
        for other_ref in (first_ref, second_ref):
            other = [other_ref[:, i * width + at : i * width + at + LANES] for i in range(4)]
            two_query, two_key, two_value, two_cot = (two_heads(block, masks) for block in other)
            other_extra = other_ref[:, 4 * width :]
            key_grad, value_grad, _ = key_side(
                own[1],
                own[2],
                two_query,
                two_cot,
                two_extras(other_extra, pair, heads, 0),
                two_extras(other_extra, pair, heads, 3 * heads),
                constants,
                scale,
            )
            key_total += key_grad
            value_total += value_grad
            score = weights_of(own[0], own_extra, two_key, logsum_lanes, scale)
            grad = weights_of(own[3], own_extra, two_value, delta_lanes, scale)
            weight = jnp.exp2(score * (scale * math.log2(math.e)))
            query_total += dot((weight * grad).astype(BF), two_key)
        query_ref[:, lanes] = (query_total * scale).astype(BF)
        total_ref[:tokens, lanes] = part_ref[tokens : 2 * tokens, lanes] + key_total * scale
        total_ref[tokens:, lanes] = value_total
        if pair % 4 == 3:
            done = slice((pair - 3) * LANES, (pair + 1) * LANES)
            outs += fetch(
                [
                    pltpu.make_async_copy(
                        query_ref.at[:, done],
                        query_hbm.at[:, done],
                        sems.at[len(pieces) + pair // 4],
                    )
                ]
            )
    for copy in outs:
        copy.wait()


def scatter_kernel(place_ref, returned_ref, total_ref, key_hbm, value_hbm, out_ref, sems):
    tokens, width = key_hbm.shape
    outs = []
    chunk = 2 * LANES
    for i in range(width // chunk):
        lanes = slice(i * chunk, (i + 1) * chunk)
        out_ref[:, lanes] = (
            total_ref[:, lanes] + dot(place_ref[...], returned_ref[:, lanes])
        ).astype(BF)
        outs += fetch(
            [
                pltpu.make_async_copy(
                    out_ref.at[j * tokens : (j + 1) * tokens, lanes],
                    hbm.at[:, lanes],
                    sems.at[2 * i + j],
                )
                for j, hbm in enumerate((key_hbm, value_hbm))
            ]
        )
    for copy in outs:
        copy.wait()


SMEM, VMEM, HBM = pltpu.SMEM, pltpu.VMEM, pltpu.HBM


def call(kernel, ins, outs, cost, scratch, sems, name):
    run = pl.pallas_call(
        kernel,
        out_shape=tuple(space(shape, kind) for shape, kind, space in outs),
        in_specs=[pl.BlockSpec(memory_space=space) for space in ins],
        out_specs=tuple(pl.BlockSpec(memory_space=space) for _, _, space in outs),
        scratch_shapes=[pltpu.VMEM(*s) for s in scratch] + [pltpu.SemaphoreType.DMA((sems,))],
        compiler_params=pltpu.CompilerParams(vmem_limit_bytes=VMEM_LIMIT),
        cost_estimate=pl.CostEstimate(flops=cost[0], bytes_accessed=cost[1], transcendentals=0),
        name=name,
    )

    def placed(*args):
        return run(
            *(
                pltpu.with_memory_space_constraint(x, space) if space is HBM else x
                for x, space in zip(args, ins, strict=True)
            )
        )

    return placed


def swap(block, axis, first):
    size = lax.axis_size(axis)
    pairs = [(i, i + 1) for i in range(first, size - 1, 2)]
    return lax.ppermute(block, axis, pairs + [(b, a) for a, b in pairs])


def on_device(
    query_matrix,
    key_matrix,
    value_matrix,
    saved_output,
    output_grad,
    row_logsum,
    key_blocks,
    halo_rows,
):
    queries, keys, values = query_matrix[0], key_matrix[0], value_matrix[0]
    saved, cotangent, logsum = saved_output[0], output_grad[0], row_logsum[0]
    tokens, width = queries.shape
    heads = logsum.shape[0]
    domains, _, cap = halo_rows.shape
    slots = domains * 2 * cap
    me = lax.axis_index("dom").astype(jnp.int32).reshape(1)
    halo = halo_rows.transpose(0, 2, 1)
    array = tokens * width
    packed = 4 * width + LANES

    def exchange(block):
        return lax.all_to_all(
            block.reshape(domains, 2 * cap, width), "dom", split_axis=0, concat_axis=0, tiled=True
        ).reshape(slots, width)

    pack, send = call(
        front_kernel,
        (SMEM,) + (HBM,) * 7,
        (((tokens, packed), BF, VMEM), ((slots, width), BF, HBM)),
        (2 * slots * array, 20 * array),
        (
            (halo.shape, jnp.int32),
            ((tokens, width), BF),
            (logsum.shape, F32),
            ((slots, width), BF),
        ),
        8,
        "front",
    )(me, halo, queries, keys, values, cotangent, saved, logsum)
    first = swap(pack, "hour", 0)
    second = swap(pack, "hour", 1)
    received = exchange(send)
    part, back = call(
        functools.partial(halo_kernel, heads, cap),
        (SMEM, VMEM, VMEM),
        (((3 * tokens, width), F32, HBM), ((slots, width), BF, HBM)),
        (20 * tokens * array, 30 * array),
        (
            ((2 * tokens, width), BF),
            ((3 * tokens, width), F32),
            ((slots, width), BF),
        ),
        heads // 2,
        "halo",
    )(key_blocks.reshape(1), pack, received)
    returned = exchange(back)
    query_grad, total, place = call(
        functools.partial(hours_kernel, heads),
        (SMEM, HBM, VMEM, pl.ANY, pl.ANY, HBM),
        (
            ((tokens, width), BF, HBM),
            ((2 * tokens, width), F32, VMEM),
            ((2 * tokens, slots), BF, VMEM),
        ),
        (56 * tokens * array, 50 * array),
        (
            (halo.shape, jnp.int32),
            ((tokens, packed), BF),
            ((tokens, packed), BF),
            ((3 * tokens, width), F32),
            ((tokens, width), BF),
        ),
        4 + heads // 8,
        "hours",
    )(me, halo, pack, first, second, part)
    key_grad, value_grad = call(
        scatter_kernel,
        (VMEM, VMEM, VMEM),
        (((tokens, width), BF, HBM), ((tokens, width), BF, HBM)),
        (2 * slots * array, 16 * array),
        (((2 * tokens, width), BF),),
        2 * (width // (2 * LANES)),
        "scatter",
    )(place, returned, total)
    return query_grad[None], key_grad[None], value_grad[None]


def solution(mesh):
    in_specs = (
        P("hour", "dom", None),
        P("hour", "dom", None),
        P("hour", "dom", None),
        P("hour", "dom", None),
        P("hour", "dom", None),
        P("hour", None, "dom"),
        P("dom", None),
        P(),
    )
    out_specs = (P("hour", "dom", None), P("hour", "dom", None), P("hour", "dom", None))
    return jax.shard_map(
        on_device, mesh=mesh, in_specs=in_specs, out_specs=out_specs, check_vma=False
    )
```

```python
import functools
import math

import jax
import jax.numpy as jnp
from jax import lax
from jax.experimental import pallas as pl
from jax.experimental.pallas import tpu as pltpu
from jax.sharding import PartitionSpec as P

BF = jnp.bfloat16
F32 = jnp.float32
LANES = 128
VMEM_LIMIT = 24 << 20


def dot(a, b):
    return lax.dot_general(a, b, (((1,), (0,)), ((), ())), preferred_element_type=F32)


def dot_nt(a, b):
    return lax.dot_general(a, b, (((1,), (1,)), ((), ())), preferred_element_type=F32)


def dot_tn(a, b):
    return lax.dot_general(a, b, (((0,), (0,)), ((), ())), preferred_element_type=F32)


def iota(shape, dim):
    return lax.broadcasted_iota(jnp.int32, shape, dim)


def one_where(mask):
    return jnp.where(mask, 1.0, 0.0).astype(BF)


def split3(x):
    hi = x.astype(BF)
    rest = x - hi.astype(F32)
    mid = rest.astype(BF)
    return hi, mid, (rest - mid.astype(F32)).astype(BF)


def start(triples):
    copies = [pltpu.make_async_copy(*triple) for triple in triples]
    for copy in copies:
        copy.start()
    return copies


def picks(halo, me, cap, slots, tokens, by_slot):
    rows = halo.astype(F32)
    twice = jnp.concatenate([rows, rows], axis=1)
    table = twice.reshape(slots, twice.shape[2]).astype(BF)
    owners = table.shape[1]
    shape = (slots, tokens) if by_slot else (tokens, slots)
    if by_slot:
        wanted = dot(table, one_where(iota((owners, tokens), 0) == me))
    else:
        wanted = dot_nt(one_where(iota((tokens, owners), 1) == me), table)
    slot_dim = 0 if by_slot else 1
    hit = wanted.astype(jnp.int32) == iota(shape, 1 - slot_dim)
    is_key = (iota(shape, slot_dim) % (2 * cap)) < cap
    both = [one_where(hit & is_key), one_where(hit & ~is_key)]
    return jnp.concatenate(both, axis=1 - slot_dim)


def front_kernel(
    me_ref,
    halo_hbm,
    query_hbm,
    key_hbm,
    value_hbm,
    cot_hbm,
    saved_hbm,
    logsum_hbm,
    ask_ref,
    own_ref,
    extra_ref,
    send_hbm,
    halo_ref,
    saved_ref,
    logsum_ref,
    send_ref,
    sems,
):
    tokens, width = query_hbm.shape
    heads = logsum_hbm.shape[0]
    head_dim = width // heads
    slots = send_ref.shape[0]
    cap = halo_hbm.shape[1]
    pieces = [
        (halo_hbm, halo_ref),
        (key_hbm, own_ref.at[:tokens]),
        (value_hbm, own_ref.at[tokens:]),
        (cot_hbm, ask_ref.at[:, width : 2 * width]),
        (saved_hbm, saved_ref),
        (logsum_hbm, logsum_ref),
        (query_hbm, ask_ref.at[:, :width]),
    ]
    copies = start([(a, b, sems.at[i]) for i, (a, b) in enumerate(pieces)])
    copies[0].wait()
    pick = picks(halo_ref[...], me_ref[0], cap, slots, tokens, True)
    copies[1].wait()
    copies[2].wait()
    send_ref[...] = dot(pick, own_ref[...]).astype(BF)
    outs = start([(send_ref, send_hbm, sems.at[len(pieces)])])
    for copy in copies[3:]:
        copy.wait()
    product = ask_ref[:, width : 2 * width].astype(F32) * saved_ref[...].astype(F32)
    high = product.astype(BF)
    low = (product - high.astype(F32)).astype(BF)
    member = one_where(iota((heads, width), 1) // head_dim == iota((heads, width), 0))
    delta = dot_nt(member, high) + dot_nt(member, low)
    parts = [p.astype(F32) for p in split3(logsum_ref[...]) + split3(delta)]
    parts.append(jnp.zeros((LANES - 6 * heads, tokens), F32))
    extra_ref[...] = jnp.concatenate(parts, axis=0).T.astype(BF)
    ask_ref[:, 2 * width :] = extra_ref[...]
    for copy in outs:
        copy.wait()


def extra_mask(head, heads, first):
    lane = iota((16, LANES), 1)
    inside = (lane >= first) & (lane < first + 3 * heads)
    return one_where(inside & (lane % heads == head))


def rows_of(pattern, tokens):
    return jnp.concatenate([pattern] * (tokens // pattern.shape[0]), axis=0)


def half_masks(tokens, head_dim):
    low = one_where(iota((16, LANES), 1) < head_dim)
    high = one_where(iota((16, LANES), 1) >= head_dim)
    return rows_of(low, tokens), rows_of(high, tokens)


def pair_dots(rows, row_extra, columns):
    return tuple(
        dot_nt(jnp.concatenate([row, extra], axis=1), column)
        for row, extra, column in zip(rows, row_extra, columns, strict=True)
    )


def pair_weights(dots, scale):
    score, grad = dots
    weight = jnp.exp2(score * (scale * math.log2(math.e)))
    return weight.astype(BF), (weight * grad).astype(BF)


def staged(count, first, second):
    ahead = first(0)
    for pair in range(count):
        now, ahead = ahead, first(pair + 1) if pair + 1 < count else None
        second(pair, now)


def minus_constants(rows, scale):
    return jnp.full((rows, LANES), -1.0 / scale, BF), jnp.full((rows, LANES), -1.0, BF)


def asking(query, cot, extra, pair, heads, masks):
    two_query, two_cot = two_heads(query, masks), two_heads(cot, masks)
    columns = (
        jnp.concatenate([two_query, two_extras(extra, pair, heads, 0)], axis=1),
        jnp.concatenate([two_cot, two_extras(extra, pair, heads, 3 * heads)], axis=1),
    )
    return two_query, two_cot, columns


def diagonal(product, tokens, head_dim):
    return jnp.concatenate([product[:head_dim, :tokens], product[head_dim:, tokens:]], axis=0)


def two_heads(block, masks):
    return jnp.concatenate([block * masks[0], block * masks[1]], axis=0)


def two_extras(extra, pair, heads, first):
    tokens = extra.shape[0]
    return jnp.concatenate(
        [extra * rows_of(extra_mask(2 * pair + i, heads, first), tokens) for i in (0, 1)], axis=0
    )


def spread(slots, cap, by_slot):
    half = slots // 2
    shape = (slots, half) if by_slot else (half, slots)
    row, column = iota(shape, 0 if by_slot else 1), iota(shape, 1 if by_slot else 0)
    owner, place = row // (2 * cap), row % (2 * cap)
    keys = one_where((place < cap) & (column == owner * cap + place))
    values = one_where((place >= cap) & (column == owner * cap + place - cap))
    return jnp.concatenate([keys, values], axis=1 if by_slot else 0)


def halo_kernel(
    heads,
    cap,
    block_ref,
    ask_ref,
    own_ref,
    recv_ref,
    part_hbm,
    low_hbm,
    pool_hbm,
    back_hbm,
    pool,
    part,
    low,
    back,
    sems,
):
    tokens = ask_ref.shape[0]
    slots, width = recv_ref.shape
    head_dim = width // heads
    scale = head_dim**-0.5
    local = block_ref[0] == 0

    @pl.when(local)
    def _():
        pool[...] = own_ref[...]

    @pl.when(jnp.logical_not(local))
    def _():
        pool[...] = dot(spread(slots, cap, False), recv_ref[...]).astype(BF)

    outs = start([(pool.at[:tokens], pool_hbm, sems.at[0])])
    masks = half_masks(tokens, head_dim)
    constants = minus_constants(tokens, scale)
    layout = spread(slots, cap, True)
    to_own = jnp.where(local, 1.0, 0.0)
    to_halo = 1.0 - to_own
    held = {}

    def first(pair):
        at = pair * LANES
        query, cot = ask_ref[:, at : at + LANES], ask_ref[:, width + at : width + at + LANES]
        two_query, two_cot, columns = asking(
            query, cot, ask_ref[:, 2 * width :], pair, heads, masks
        )
        rows = pool[:tokens, at : at + LANES], pool[tokens:, at : at + LANES]
        return two_query, two_cot, pair_dots(rows, constants, columns)

    def second(pair, stage):
        at = pair * LANES
        two_query, two_cot, dots = stage
        weight_low, grad_low = pair_weights(dots, scale)
        low[:, 2 * at : 2 * at + 2 * LANES] = grad_low
        key_grad = dot(grad_low, two_query) * scale
        value_grad = dot(weight_low, two_cot)
        part[:tokens, at : at + LANES] = key_grad * to_own
        part[tokens:, at : at + LANES] = value_grad * to_own
        held[pair] = jnp.concatenate([key_grad * to_halo, value_grad * to_halo], axis=0).astype(BF)
        if pair % 2 == 0:
            return
        lanes = slice(at - LANES, at + LANES)
        wide = slice(2 * (at - LANES), 2 * (at + LANES))
        both = jnp.concatenate([held[pair - 1], held[pair]], axis=1)
        back[:, lanes] = dot(layout, both).astype(BF)
        index = 3 * (pair // 2)
        outs.extend(
            start(
                [
                    (back.at[:, lanes], back_hbm.at[:, lanes], sems.at[index + 1]),
                    (part.at[:, lanes], part_hbm.at[:, lanes], sems.at[index + 2]),
                    (low.at[:, wide], low_hbm.at[:, wide], sems.at[index + 3]),
                ]
            )
        )

    staged(heads // 2, first, second)
    for copy in outs:
        copy.wait()


def key_kernel(
    heads,
    me_ref,
    halo_hbm,
    own_ref,
    first_hbm,
    second_hbm,
    part_hbm,
    low_hbm,
    pool_hbm,
    total_ref,
    place_ref,
    query_hbm,
    halo_ref,
    asked,
    part,
    low,
    pool,
    query_part,
    sems,
):
    tokens, width = pool_hbm.shape
    head_dim = width // heads
    scale = head_dim**-0.5
    copies = start(
        [
            (halo_hbm, halo_ref, sems.at[0]),
            (first_hbm, asked.at[:tokens], sems.at[1]),
            (second_hbm, asked.at[tokens:], sems.at[2]),
            (low_hbm, low, sems.at[3]),
            (pool_hbm, pool, sems.at[4]),
            (part_hbm, part, sems.at[5]),
        ]
    )
    copies[0].wait()
    place_ref[...] = picks(
        halo_ref[...], me_ref[0], halo_ref.shape[1], place_ref.shape[1], tokens, False
    )
    for copy in copies[1:3]:
        copy.wait()
    masks = half_masks(tokens, head_dim)
    extra = asked[:, 2 * width :]

    def first(pair):
        at = pair * LANES
        lanes = slice(at, at + LANES)
        columns = tuple(
            jnp.concatenate(
                [
                    two_heads(own_ref[row : row + tokens, lanes], masks),
                    jnp.concatenate(
                        [
                            rows_of(extra_mask(2 * pair + i, heads, lane) * BF(by), tokens)
                            for i in (0, 1)
                        ],
                        axis=0,
                    ),
                ],
                axis=1,
            )
            for row, lane, by in ((0, 0, -1.0 / scale), (tokens, 3 * heads, -1.0))
        )
        query, cot = asked[:, lanes], asked[:, width + at : width + at + LANES]
        return query, cot, pair_dots((query, cot), (extra, extra), columns)

    def second(pair, stage):
        at = pair * LANES
        lanes = slice(at, at + LANES)
        query, cot, dots = stage
        weight_low, grad_low = pair_weights(dots, scale)
        if pair == 0:
            for copy in copies[3:]:
                copy.wait()
        key_grad = diagonal(dot_tn(query, grad_low), tokens, head_dim)
        value_grad = diagonal(dot_tn(cot, weight_low), tokens, head_dim)
        total_ref[:tokens, lanes] = part[:tokens, lanes] + (key_grad * scale).T
        total_ref[tokens:, lanes] = part[tokens:, lanes] + value_grad.T
        query_part[lanes] = diagonal(
            dot_tn(pool[:, lanes], low[:, 2 * at : 2 * at + 2 * LANES]), tokens, head_dim
        )

    staged(heads // 2, first, second)
    for copy in start([(query_part, query_hbm, sems.at[6])]):
        copy.wait()


def query_kernel(
    heads,
    extra_ref,
    own_query_hbm,
    own_cot_hbm,
    first_hbm,
    second_hbm,
    part_hbm,
    query_hbm,
    query_own,
    cot_own,
    listed,
    part,
    query_ref,
    sems,
):
    tokens, width = query_hbm.shape
    head_dim = width // heads
    scale = head_dim**-0.5
    halves = [slice(i * width // 2, (i + 1) * width // 2) for i in (0, 1)]
    own = start([(own_query_hbm, query_own, sems.at[9]), (own_cot_hbm, cot_own, sems.at[10])])
    copies = [
        start(
            [
                (hbm.at[row : row + tokens, half], listed.at[to : to + tokens, half], sems.at[at])
                for at, (hbm, row, to) in enumerate(
                    (
                        (first_hbm, 0, 0),
                        (second_hbm, 0, tokens),
                        (first_hbm, tokens, 2 * tokens),
                        (second_hbm, tokens, 3 * tokens),
                    ),
                    4 * i,
                )
            ]
        )
        for i, half in enumerate(halves)
    ]
    copies[0] += start([(part_hbm, part, sems.at[8])])
    for copy in own:
        copy.wait()
    masks = half_masks(tokens, head_dim)
    constants = minus_constants(2 * tokens, scale)
    outs = []

    def first(pair):
        if pair % (heads // 4) == 0:
            for copy in copies[pair // (heads // 4)][:4]:
                copy.wait()
        at = pair * LANES
        lanes = slice(at, at + LANES)
        _, _, columns = asking(
            query_own[:, lanes], cot_own[:, lanes], extra_ref[...], pair, heads, masks
        )
        keys = listed[: 2 * tokens, lanes]
        return keys, pair_dots((keys, listed[2 * tokens :, lanes]), constants, columns)

    def second(pair, stage):
        lanes = slice(pair * LANES, (pair + 1) * LANES)
        keys, dots = stage
        _, grad_low = pair_weights(dots, scale)
        if pair == 0:
            copies[0][4].wait()
        grad = diagonal(dot_tn(keys, grad_low), tokens, head_dim) + part[lanes]
        query_ref[:, lanes] = (grad * scale).T.astype(BF)
        if pair % 4 == 3:
            done = slice((pair - 3) * LANES, (pair + 1) * LANES)
            outs.extend(
                start([(query_ref.at[:, done], query_hbm.at[:, done], sems.at[11 + pair // 4])])
            )

    staged(heads // 2, first, second)
    for copy in outs:
        copy.wait()


def scatter_kernel(place_ref, returned_ref, total_ref, key_hbm, value_hbm, out_ref, sems):
    tokens, width = key_hbm.shape
    outs = []
    chunk = 2 * LANES
    for i in range(width // chunk):
        lanes = slice(i * chunk, (i + 1) * chunk)
        out_ref[:, lanes] = (
            total_ref[:, lanes] + dot(place_ref[...], returned_ref[:, lanes])
        ).astype(BF)
        outs += start(
            [
                (
                    out_ref.at[j * tokens : (j + 1) * tokens, lanes],
                    hbm.at[:, lanes],
                    sems.at[2 * i + j],
                )
                for j, hbm in enumerate((key_hbm, value_hbm))
            ]
        )
    for copy in outs:
        copy.wait()


SMEM, VMEM, HBM = pltpu.SMEM, pltpu.VMEM, pltpu.HBM


def call(kernel, ins, outs, cost, scratch, sems, name):
    run = pl.pallas_call(
        kernel,
        out_shape=tuple(space(shape, kind) for shape, kind, space in outs),
        in_specs=[pl.BlockSpec(memory_space=space) for space in ins],
        out_specs=tuple(pl.BlockSpec(memory_space=space) for _, _, space in outs),
        scratch_shapes=[pltpu.VMEM(*s) for s in scratch] + [pltpu.SemaphoreType.DMA((sems,))],
        compiler_params=pltpu.CompilerParams(
            vmem_limit_bytes=VMEM_LIMIT
        ),
        cost_estimate=pl.CostEstimate(flops=cost[0], bytes_accessed=cost[1], transcendentals=0),
        name=name,
    )

    def placed(*args):
        return run(
            *(
                pltpu.with_memory_space_constraint(x, space) if space is HBM else x
                for x, space in zip(args, ins, strict=True)
            )
        )

    return placed


def swap(block, axis, first):
    size = lax.axis_size(axis)
    pairs = [(i, i + 1) for i in range(first, size - 1, 2)]
    return lax.ppermute(block, axis, pairs + [(b, a) for a, b in pairs])


def on_device(
    query_matrix,
    key_matrix,
    value_matrix,
    saved_output,
    output_grad,
    row_logsum,
    key_blocks,
    halo_rows,
):
    queries, keys, values = query_matrix[0], key_matrix[0], value_matrix[0]
    saved, cotangent, logsum = saved_output[0], output_grad[0], row_logsum[0]
    tokens, width = queries.shape
    heads = logsum.shape[0]
    domains, _, cap = halo_rows.shape
    slots = domains * 2 * cap
    me = lax.axis_index("dom").astype(jnp.int32).reshape(1)
    halo = halo_rows.transpose(0, 2, 1)
    array = tokens * width
    asked = 2 * width + LANES

    def exchange(block):
        return lax.all_to_all(
            block.reshape(domains, 2 * cap, width), "dom", split_axis=0, concat_axis=0, tiled=True
        ).reshape(slots, width)

    ask, own, extra, send = call(
        front_kernel,
        (SMEM,) + (HBM,) * 7,
        (
            ((tokens, asked), BF, VMEM),
            ((2 * tokens, width), BF, VMEM),
            ((tokens, LANES), BF, VMEM),
            ((slots, width), BF, HBM),
        ),
        (2 * slots * array, 20 * array),
        (
            (halo.shape, jnp.int32),
            ((tokens, width), BF),
            (logsum.shape, F32),
            ((slots, width), BF),
        ),
        8,
        "front",
    )(me, halo, queries, keys, values, cotangent, saved, logsum)
    with jax.named_scope("halo_out"):
        received = exchange(send)
    with jax.named_scope("ask_first"):
        ask_first = swap(ask, "hour", 0)
    with jax.named_scope("ask_second"):
        ask_second = swap(ask, "hour", 1)
    with jax.named_scope("own_first"):
        own_first = swap(own, "hour", 0)
    with jax.named_scope("own_second"):
        own_second = swap(own, "hour", 1)
    part, low, pool, back = call(
        functools.partial(halo_kernel, heads, cap),
        (SMEM, VMEM, VMEM, VMEM),
        (
            ((2 * tokens, width), F32, HBM),
            ((tokens, 2 * width), BF, HBM),
            ((tokens, width), BF, HBM),
            ((slots, width), BF, HBM),
        ),
        (20 * tokens * array, 30 * array),
        (
            ((2 * tokens, width), BF),
            ((2 * tokens, width), F32),
            ((tokens, 2 * width), BF),
            ((slots, width), BF),
        ),
        1 + 3 * (heads // 4),
        "halo",
    )(key_blocks.reshape(1), ask, own, received)
    with jax.named_scope("halo_back"):
        returned = exchange(back)
    total, place, query_part = call(
        functools.partial(key_kernel, heads),
        (SMEM, HBM, VMEM, pl.ANY, pl.ANY, HBM, HBM, HBM),
        (
            ((2 * tokens, width), F32, VMEM),
            ((2 * tokens, slots), BF, VMEM),
            ((width, tokens), F32, HBM),
        ),
        (36 * tokens * array, 40 * array),
        (
            (halo.shape, jnp.int32),
            ((2 * tokens, asked), BF),
            ((2 * tokens, width), F32),
            ((tokens, 2 * width), BF),
            ((tokens, width), BF),
            ((width, tokens), F32),
        ),
        7,
        "hour_keys",
    )(me, halo, own, ask_first, ask_second, part, low, pool)
    (query_grad,) = call(
        functools.partial(query_kernel, heads),
        (VMEM, HBM, HBM, pl.ANY, pl.ANY, HBM),
        (((tokens, width), BF, HBM),),
        (24 * tokens * array, 20 * array),
        (
            ((tokens, width), BF),
            ((tokens, width), BF),
            ((4 * tokens, width), BF),
            ((width, tokens), F32),
            ((tokens, width), BF),
        ),
        11 + heads // 8,
        "hour_queries",
    )(extra, queries, cotangent, own_first, own_second, query_part)
    key_grad, value_grad = call(
        scatter_kernel,
        (VMEM, VMEM, VMEM),
        (((tokens, width), BF, HBM), ((tokens, width), BF, HBM)),
        (2 * slots * array, 16 * array),
        (((2 * tokens, width), BF),),
        2 * (width // (2 * LANES)),
        "scatter",
    )(place, returned, total)
    return query_grad[None], key_grad[None], value_grad[None]


def solution(mesh):
    in_specs = (
        P("hour", "dom", None),
        P("hour", "dom", None),
        P("hour", "dom", None),
        P("hour", "dom", None),
        P("hour", "dom", None),
        P("hour", None, "dom"),
        P("dom", None),
        P(),
    )
    out_specs = (P("hour", "dom", None), P("hour", "dom", None), P("hour", "dom", None))
    return jax.shard_map(
        on_device, mesh=mesh, in_specs=in_specs, out_specs=out_specs, check_vma=False
    )
```

```python
import functools
import math

import jax
import jax.numpy as jnp
from jax import lax
from jax.experimental import pallas as pl
from jax.experimental.pallas import tpu as pltpu
from jax.sharding import PartitionSpec as P


BF = jnp.bfloat16
F32 = jnp.float32
LANES = 128
VMEM_LIMIT = 24 << 20


def dot(a, b):
    return lax.dot_general(a, b, (((1,), (0,)), ((), ())), preferred_element_type=F32)


def dot_nt(a, b):
    return lax.dot_general(a, b, (((1,), (1,)), ((), ())), preferred_element_type=F32)


def dot_tn(a, b):
    return lax.dot_general(a, b, (((0,), (0,)), ((), ())), preferred_element_type=F32)


def iota(shape, dim):
    return lax.broadcasted_iota(jnp.int32, shape, dim)


def one_where(mask):
    return jnp.where(mask, 1.0, 0.0).astype(BF)


def split3(x):
    hi = x.astype(BF)
    rest = x - hi.astype(F32)
    mid = rest.astype(BF)
    return hi, mid, (rest - mid.astype(F32)).astype(BF)


def start(triples):
    copies = [pltpu.make_async_copy(*triple) for triple in triples]
    for copy in copies:
        copy.start()
    return copies


def picks(halo, me, tokens, by_slot):
    rows = halo.astype(F32)
    table = rows.reshape(rows.shape[0] * rows.shape[1], rows.shape[2]).astype(BF)
    slots, owners = table.shape
    if by_slot:
        wanted = dot(table, one_where(iota((owners, tokens), 0) == me))
        return one_where(wanted.astype(jnp.int32) == iota((slots, tokens), 1))
    wanted = dot_nt(one_where(iota((tokens, owners), 1) == me), table)
    return one_where(wanted.astype(jnp.int32) == iota((tokens, slots), 0))


def front_kernel(
    me_ref,
    halo_hbm,
    query_hbm,
    key_hbm,
    value_hbm,
    cot_hbm,
    saved_hbm,
    logsum_hbm,
    pack_ref,
    extra_ref,
    send_hbm,
    halo_ref,
    saved_ref,
    logsum_ref,
    send_ref,
    sems,
):
    tokens, width = query_hbm.shape
    heads = logsum_hbm.shape[0]
    head_dim = width // heads
    domains, cap, _ = send_ref.shape
    pieces = [
        (halo_hbm, halo_ref),
        (key_hbm, pack_ref.at[:, 2 * width : 3 * width]),
        (value_hbm, pack_ref.at[:, 3 * width : 4 * width]),
        (cot_hbm, pack_ref.at[:, width : 2 * width]),
        (saved_hbm, saved_ref),
        (logsum_hbm, logsum_ref),
        (query_hbm, pack_ref.at[:, :width]),
    ]
    copies = start([(a, b, sems.at[i]) for i, (a, b) in enumerate(pieces)])
    copies[0].wait()
    pick = picks(halo_ref[...], me_ref[0], tokens, True)
    for i in (0, 1):
        copies[1 + i].wait()
        rows = dot(pick, pack_ref[:, (2 + i) * width : (3 + i) * width])
        send_ref[:, :, i * width : (i + 1) * width] = rows.reshape(domains, cap, width).astype(BF)
    outs = start([(send_ref, send_hbm, sems.at[len(pieces)])])
    for copy in copies[3:]:
        copy.wait()
    product = pack_ref[:, width : 2 * width].astype(F32) * saved_ref[...].astype(F32)
    high = product.astype(BF)
    low = (product - high.astype(F32)).astype(BF)
    member = one_where(iota((heads, width), 1) // head_dim == iota((heads, width), 0))
    delta = dot_nt(member, high) + dot_nt(member, low)
    parts = [p.astype(F32) for p in split3(logsum_ref[...]) + split3(delta)]
    parts.append(jnp.zeros((LANES - 6 * heads, tokens), F32))
    extra_ref[...] = jnp.concatenate(parts, axis=0).T.astype(BF)
    pack_ref[:, 4 * width :] = extra_ref[...]
    for copy in outs:
        copy.wait()


def extra_mask(head, heads, first):
    lane = iota((16, LANES), 1)
    inside = (lane >= first) & (lane < first + 3 * heads)
    return one_where(inside & (lane % heads == head))


def rows_of(pattern, tokens):
    return jnp.concatenate([pattern] * (tokens // pattern.shape[0]), axis=0)


def half_masks(tokens, head_dim):
    low = one_where(iota((16, LANES), 1) < head_dim)
    high = one_where(iota((16, LANES), 1) >= head_dim)
    return rows_of(low, tokens), rows_of(high, tokens)


def pair_dots(rows, row_extra, columns):
    return tuple(
        dot_nt(jnp.concatenate([row, extra], axis=1), column)
        for row, extra, column in zip(rows, row_extra, columns, strict=True)
    )


def pair_weights(dots, scale):
    score, grad = dots
    weight = jnp.exp2(score * (scale * math.log2(math.e)))
    return weight.astype(BF), (weight * grad).astype(BF)


def staged(count, first, second):
    ahead = first(0)
    for pair in range(count):
        now, ahead = ahead, first(pair + 1) if pair + 1 < count else None
        second(pair, now)


def minus_constants(rows, scale):
    return jnp.full((rows, LANES), -1.0 / scale, BF), jnp.full((rows, LANES), -1.0, BF)


def asking(query, cot, extra, pair, heads, masks):
    two_query, two_cot = two_heads(query, masks), two_heads(cot, masks)
    columns = (
        jnp.concatenate([two_query, two_extras(extra, pair, heads, 0)], axis=1),
        jnp.concatenate([two_cot, two_extras(extra, pair, heads, 3 * heads)], axis=1),
    )
    return two_query, two_cot, columns


def diagonal(product, tokens, head_dim):
    return jnp.concatenate([product[:head_dim, :tokens], product[head_dim:, tokens:]], axis=0)


def two_heads(block, masks):
    return jnp.concatenate([block * masks[0], block * masks[1]], axis=0)


def two_extras(extra, pair, heads, first):
    tokens = extra.shape[0]
    return jnp.concatenate(
        [extra * rows_of(extra_mask(2 * pair + i, heads, first), tokens) for i in (0, 1)], axis=0
    )


def halo_kernel(
    heads,
    block_ref,
    pack_ref,
    recv_ref,
    part_hbm,
    low_hbm,
    pool_hbm,
    back_hbm,
    pool,
    part,
    low,
    back,
    sems,
):
    tokens = pack_ref.shape[0]
    domains, cap, wide = recv_ref.shape
    width = wide // 2
    head_dim = width // heads
    scale = head_dim**-0.5
    local = block_ref[0] == 0

    @pl.when(local)
    def _():
        pool[:tokens] = pack_ref[:, 2 * width : 3 * width]
        pool[tokens:] = pack_ref[:, 3 * width : 4 * width]

    @pl.when(jnp.logical_not(local))
    def _():
        for i in (0, 1):
            rows = recv_ref[:, :, i * width : (i + 1) * width].astype(F32)
            pool[i * tokens : (i + 1) * tokens] = rows.reshape(domains * cap, width).astype(BF)

    outs = start([(pool.at[:tokens], pool_hbm, sems.at[0])])
    masks = half_masks(tokens, head_dim)
    constants = minus_constants(tokens, scale)
    to_own = jnp.where(local, 1.0, 0.0)
    to_halo = 1.0 - to_own

    def first(pair):
        at = pair * LANES
        query, cot = pack_ref[:, at : at + LANES], pack_ref[:, width + at : width + at + LANES]
        two_query, two_cot, columns = asking(
            query, cot, pack_ref[:, 4 * width :], pair, heads, masks
        )
        rows = pool[:tokens, at : at + LANES], pool[tokens:, at : at + LANES]
        return two_query, two_cot, pair_dots(rows, constants, columns)

    def second(pair, stage):
        at = pair * LANES
        two_query, two_cot, dots = stage
        weight_low, grad_low = pair_weights(dots, scale)
        low[:, 2 * at : 2 * at + 2 * LANES] = grad_low
        key_grad = dot(grad_low, two_query) * scale
        value_grad = dot(weight_low, two_cot)
        part[:tokens, at : at + LANES] = key_grad * to_own
        part[tokens:, at : at + LANES] = value_grad * to_own
        for i, grad in enumerate((key_grad, value_grad)):
            rows = (grad * to_halo).reshape(domains, cap, LANES)
            back[:, :, i * width + at : i * width + at + LANES] = rows.astype(BF)
        if pair % 4 != 3:
            return
        lanes = slice(at - 3 * LANES, at + LANES)
        wide = slice(2 * (at - 3 * LANES), 2 * (at + LANES))
        beside = slice(width + at - 3 * LANES, width + at + LANES)
        index = 4 * (pair // 4)
        outs.extend(
            start(
                [
                    (back.at[:, :, lanes], back_hbm.at[:, :, lanes], sems.at[index + 1]),
                    (back.at[:, :, beside], back_hbm.at[:, :, beside], sems.at[index + 2]),
                    (part.at[:, lanes], part_hbm.at[:, lanes], sems.at[index + 3]),
                    (low.at[:, wide], low_hbm.at[:, wide], sems.at[index + 4]),
                ]
            )
        )

    staged(heads // 2, first, second)
    for copy in outs:
        copy.wait()


def own_keys(keys, values, pair, heads, masks, scale):
    tokens = keys.shape[0]
    return tuple(
        jnp.concatenate(
            [
                two_heads(block, masks),
                jnp.concatenate(
                    [rows_of(extra_mask(2 * pair + i, heads, at) * BF(by), tokens) for i in (0, 1)],
                    axis=0,
                ),
            ],
            axis=1,
        )
        for block, at, by in ((keys, 0, -1.0 / scale), (values, 3 * heads, -1.0))
    )


def both_sides(heads, width, pack_ref, other, ready, before, finish):
    tokens = pack_ref.shape[0]
    head_dim = width // heads
    scale = head_dim**-0.5
    masks = half_masks(tokens, head_dim)
    constants = minus_constants(tokens, scale)

    def blocks(ref, pair):
        starts = [i * width + pair * LANES for i in range(4)]
        return [ref[:, at : at + LANES] for at in starts]

    def first(pair):
        ready(pair)
        query, cot, key, value = blocks(pack_ref, pair)
        their_query, their_cot, their_key, their_value = blocks(other, pair)
        extra = other[:, 4 * width :]
        _, _, columns = asking(query, cot, pack_ref[:, 4 * width :], pair, heads, masks)
        under = pair_dots(
            (their_query, their_cot), (extra, extra), own_keys(key, value, pair, heads, masks, scale)
        )
        over = pair_dots((their_key, their_value), constants, columns)
        return under, over

    def second(pair, stage):
        under, over = stage
        their_query, their_cot, their_key, _ = blocks(other, pair)
        weight_low, grad_low = pair_weights(under, scale)
        _, query_low = pair_weights(over, scale)
        keys, lows = before(pair, their_key, query_low)
        query_grad = diagonal(dot_tn(keys, lows), tokens, head_dim)
        key_grad = diagonal(dot_tn(their_query, grad_low), tokens, head_dim)
        value_grad = diagonal(dot_tn(their_cot, weight_low), tokens, head_dim)
        finish(pair, (query_grad * scale).T, (key_grad * scale).T, value_grad.T)

    staged(heads // 2, first, second)


def early_kernel(
    heads,
    me_ref,
    halo_hbm,
    pack_ref,
    other_hbm,
    low_hbm,
    pool_hbm,
    part_hbm,
    grads_hbm,
    place_ref,
    halo_ref,
    other,
    low,
    pool,
    part,
    grads,
    sems,
):
    tokens, width = pool_hbm.shape
    copies = start(
        [
            (other_hbm, other, sems.at[0]),
            (low_hbm, low, sems.at[1]),
            (pool_hbm, pool, sems.at[2]),
            (part_hbm, part, sems.at[3]),
            (halo_hbm, halo_ref, sems.at[4]),
        ]
    )
    copies[4].wait()
    place_ref[...] = picks(halo_ref[...], me_ref[0], tokens, False)
    copies[0].wait()
    outs = []

    def ready(pair):
        pass

    def before(pair, keys, query_low):
        if pair == 0:
            for copy in copies[1:4]:
                copy.wait()
        at = pair * LANES
        listed = low[:, 2 * at : 2 * at + 2 * LANES]
        return (
            jnp.concatenate([keys, pool[:, at : at + LANES]], axis=0),
            jnp.concatenate([query_low, listed], axis=0),
        )

    def finish(pair, query_grad, key_grad, value_grad):
        lanes = slice(pair * LANES, (pair + 1) * LANES)
        grads[:tokens, lanes] = query_grad
        grads[tokens : 2 * tokens, lanes] = part[:tokens, lanes] + key_grad
        grads[2 * tokens :, lanes] = part[tokens:, lanes] + value_grad
        if pair % 4 == 3:
            done = slice((pair - 3) * LANES, (pair + 1) * LANES)
            outs.extend(
                start([(grads.at[:, done], grads_hbm.at[:, done], sems.at[5 + pair // 4])])
            )

    both_sides(heads, width, pack_ref, other, ready, before, finish)
    for copy in outs:
        copy.wait()


def late_kernel(
    heads,
    own_query_hbm,
    own_cot_hbm,
    own_key_hbm,
    own_value_hbm,
    extra_ref,
    other_hbm,
    grads_hbm,
    total_ref,
    query_hbm,
    own,
    other,
    grads,
    query_ref,
    sems,
):
    tokens, width = query_hbm.shape
    half = width // 2

    def load(side):
        owned = (own_query_hbm, own_cot_hbm, own_key_hbm, own_value_hbm)
        part = slice(side * half, (side + 1) * half)
        blocks = [slice(i * width + side * half, i * width + (side + 1) * half) for i in range(4)]
        at = 9 * side
        triples = [
            (other_hbm.at[:, block], other.at[:, block], sems.at[at + i])
            for i, block in enumerate(blocks)
        ]
        triples += [
            (hbm.at[:, part], own.at[:, block], sems.at[at + 4 + i])
            for i, (hbm, block) in enumerate(zip(owned, blocks, strict=True))
        ]
        triples.append((grads_hbm.at[:, part], grads.at[:, part], sems.at[at + 8]))
        return start(triples)

    beside = slice(4 * width, 4 * width + LANES)
    extra = start([(other_hbm.at[:, beside], other.at[:, beside], sems.at[18])])
    copies = load(0), load(1)
    own[:, 4 * width :] = extra_ref[...]
    outs = []

    def ready(pair):
        if pair == 0:
            for copy in extra + copies[0][:8]:
                copy.wait()
        if pair == heads // 4:
            for copy in copies[1][:8]:
                copy.wait()

    def before(pair, keys, query_low):
        if pair == 0:
            copies[0][8].wait()
            copies[1][8].wait()
        return keys, query_low

    def finish(pair, query_grad, key_grad, value_grad):
        lanes = slice(pair * LANES, (pair + 1) * LANES)
        query_ref[:, lanes] = (grads[:tokens, lanes] + query_grad).astype(BF)
        total_ref[:tokens, lanes] = grads[tokens : 2 * tokens, lanes] + key_grad
        total_ref[tokens:, lanes] = grads[2 * tokens :, lanes] + value_grad
        if pair % 4 == 3:
            done = slice((pair - 3) * LANES, (pair + 1) * LANES)
            outs.extend(
                start([(query_ref.at[:, done], query_hbm.at[:, done], sems.at[19 + pair // 4])])
            )

    both_sides(heads, width, own, other, ready, before, finish)
    for copy in outs:
        copy.wait()


def scatter_kernel(place_ref, returned_ref, total_ref, key_hbm, value_hbm, out_ref, sems):
    tokens, width = key_hbm.shape
    domains, cap, _ = returned_ref.shape
    outs = []
    chunk = 4 * LANES
    for i in range(width // chunk):
        for j, hbm in enumerate((key_hbm, value_hbm)):
            lanes = slice(i * chunk, (i + 1) * chunk)
            rows = slice(j * tokens, (j + 1) * tokens)
            at = j * width + i * chunk
            returned = returned_ref[:, :, at : at + chunk].astype(F32)
            returned = returned.reshape(domains * cap, chunk).astype(BF)
            out_ref[rows, lanes] = (total_ref[rows, lanes] + dot(place_ref[...], returned)).astype(BF)
            outs += start([(out_ref.at[rows, lanes], hbm.at[:, lanes], sems.at[2 * i + j])])
    for copy in outs:
        copy.wait()


SMEM, VMEM, HBM = pltpu.SMEM, pltpu.VMEM, pltpu.HBM


def call(kernel, ins, outs, cost, scratch, sems):
    run = pl.pallas_call(
        kernel,
        out_shape=tuple(space(shape, kind) for shape, kind, space in outs),
        in_specs=[pl.BlockSpec(memory_space=space) for space in ins],
        out_specs=tuple(pl.BlockSpec(memory_space=space) for _, _, space in outs),
        scratch_shapes=[pltpu.VMEM(*s) for s in scratch] + [pltpu.SemaphoreType.DMA((sems,))],
        compiler_params=pltpu.CompilerParams(vmem_limit_bytes=VMEM_LIMIT),
        cost_estimate=pl.CostEstimate(flops=cost[0], bytes_accessed=cost[1], transcendentals=0),
    )

    def placed(*args):
        return run(
            *(
                pltpu.with_memory_space_constraint(x, space) if space is HBM else x
                for x, space in zip(args, ins, strict=True)
            )
        )

    return placed


def swap(block, axis, first):
    size = lax.axis_size(axis)
    pairs = [(i, i + 1) for i in range(first, size - 1, 2)]
    return lax.ppermute(block, axis, pairs + [(b, a) for a, b in pairs])


def backward(
    query_matrix,
    key_matrix,
    value_matrix,
    saved_output,
    output_grad,
    row_logsum,
    key_blocks,
    halo_rows,
):
    queries, keys, values = query_matrix[0], key_matrix[0], value_matrix[0]
    saved, cotangent, logsum = saved_output[0], output_grad[0], row_logsum[0]
    tokens, width = queries.shape
    heads = logsum.shape[0]
    domains, _, cap = halo_rows.shape
    slots = domains * cap
    me = lax.axis_index("dom").astype(jnp.int32).reshape(1)
    halo = halo_rows.transpose(0, 2, 1)
    array = tokens * width
    packed = 4 * width + LANES

    def exchange(block):
        return lax.all_to_all(block, "dom", split_axis=0, concat_axis=0, tiled=True)

    pack, extra, send = call(
        front_kernel,
        (SMEM,) + (HBM,) * 7,
        (
            ((tokens, packed), BF, VMEM),
            ((tokens, LANES), BF, VMEM),
            ((domains, cap, 2 * width), BF, HBM),
        ),
        (2 * slots * array, 20 * array),
        (
            (halo.shape, jnp.int32),
            ((tokens, width), BF),
            (logsum.shape, F32),
            ((domains, cap, 2 * width), BF),
        ),
        8,
    )(me, halo, queries, keys, values, cotangent, saved, logsum)
    received = exchange(send)
    odd = swap(pack, "hour", 1)
    even = swap(pack, "hour", 0)
    part, low, pool, back = call(
        functools.partial(halo_kernel, heads),
        (SMEM, VMEM, VMEM),
        (
            ((2 * tokens, width), F32, HBM),
            ((tokens, 2 * width), BF, HBM),
            ((tokens, width), BF, HBM),
            ((domains, cap, 2 * width), BF, HBM),
        ),
        (20 * tokens * array, 30 * array),
        (
            ((2 * tokens, width), BF),
            ((2 * tokens, width), F32),
            ((tokens, 2 * width), BF),
            ((domains, cap, 2 * width), BF),
        ),
        1 + heads // 2,
    )(key_blocks.reshape(1), pack, received)
    returned = exchange(back)
    grads, place = call(
        functools.partial(early_kernel, heads),
        (SMEM, HBM, VMEM, pl.ANY, HBM, HBM, HBM),
        (((3 * tokens, width), F32, HBM), ((tokens, slots), BF, VMEM)),
        (30 * tokens * array, 40 * array),
        (
            (halo.shape, jnp.int32),
            ((tokens, packed), BF),
            ((tokens, 2 * width), BF),
            ((tokens, width), BF),
            ((2 * tokens, width), F32),
            ((3 * tokens, width), F32),
        ),
        5 + heads // 8,
    )(me, halo, pack, even, low, pool, part)
    total, query_grad = call(
        functools.partial(late_kernel, heads),
        (HBM, HBM, HBM, HBM, VMEM, pl.ANY, HBM),
        (((2 * tokens, width), F32, VMEM), ((tokens, width), BF, HBM)),
        (28 * tokens * array, 40 * array),
        (
            ((tokens, packed), BF),
            ((tokens, packed), BF),
            ((3 * tokens, width), F32),
            ((tokens, width), BF),
        ),
        19 + heads // 8,
    )(queries, cotangent, keys, values, extra, odd, grads)
    key_grad, value_grad = call(
        scatter_kernel,
        (VMEM, VMEM, VMEM),
        (((tokens, width), BF, HBM), ((tokens, width), BF, HBM)),
        (2 * slots * array, 16 * array),
        (((2 * tokens, width), BF),),
        2 * (width // (4 * LANES)),
    )(place, returned, total)
    return query_grad[None], key_grad[None], value_grad[None]


def solution(mesh):
    in_specs = (
        P("hour", "dom", None),
        P("hour", "dom", None),
        P("hour", "dom", None),
        P("hour", "dom", None),
        P("hour", "dom", None),
        P("hour", None, "dom"),
        P("dom", None),
        P(),
    )
    out_specs = (P("hour", "dom", None), P("hour", "dom", None), P("hour", "dom", None))
    return jax.shard_map(
        backward, mesh=mesh, in_specs=in_specs, out_specs=out_specs, check_vma=False
    )
```

```python
import functools
import math

import jax
import jax.numpy as jnp
from jax import lax
from jax.experimental import pallas as pl
from jax.experimental.pallas import tpu as pltpu
from jax.sharding import PartitionSpec as P


BF = jnp.bfloat16
F32 = jnp.float32
LANES = 128
VMEM_LIMIT = 24 << 20


def dot(a, b):
    return lax.dot_general(a, b, (((1,), (0,)), ((), ())), preferred_element_type=F32)


def dot_nt(a, b):
    return lax.dot_general(a, b, (((1,), (1,)), ((), ())), preferred_element_type=F32)


def dot_tn(a, b):
    return lax.dot_general(a, b, (((0,), (0,)), ((), ())), preferred_element_type=F32)


def iota(shape, dim):
    return lax.broadcasted_iota(jnp.int32, shape, dim)


def one_where(mask):
    return jnp.where(mask, 1.0, 0.0).astype(BF)


def split3(x):
    hi = x.astype(BF)
    rest = x - hi.astype(F32)
    mid = rest.astype(BF)
    return hi, mid, (rest - mid.astype(F32)).astype(BF)


def start(triples):
    copies = [pltpu.make_async_copy(*triple) for triple in triples]
    for copy in copies:
        copy.start()
    return copies


def picks(halo, me, tokens, by_slot):
    rows = halo.astype(F32)
    table = rows.reshape(rows.shape[0] * rows.shape[1], rows.shape[2]).astype(BF)
    slots, owners = table.shape
    if by_slot:
        wanted = dot(table, one_where(iota((owners, tokens), 0) == me))
        return one_where(wanted.astype(jnp.int32) == iota((slots, tokens), 1))
    wanted = dot_nt(one_where(iota((tokens, owners), 1) == me), table)
    return one_where(wanted.astype(jnp.int32) == iota((tokens, slots), 0))


def front_kernel(
    me_ref,
    halo_hbm,
    query_hbm,
    key_hbm,
    value_hbm,
    cot_hbm,
    saved_hbm,
    logsum_hbm,
    pack_ref,
    extra_ref,
    send_hbm,
    halo_ref,
    saved_ref,
    logsum_ref,
    send_ref,
    sems,
):
    tokens, width = query_hbm.shape
    heads = logsum_hbm.shape[0]
    head_dim = width // heads
    domains, cap, _ = send_ref.shape
    pieces = [
        (halo_hbm, halo_ref),
        (key_hbm, pack_ref.at[:, 2 * width : 3 * width]),
        (value_hbm, pack_ref.at[:, 3 * width : 4 * width]),
        (cot_hbm, pack_ref.at[:, width : 2 * width]),
        (saved_hbm, saved_ref),
        (logsum_hbm, logsum_ref),
        (query_hbm, pack_ref.at[:, :width]),
    ]
    copies = start([(a, b, sems.at[i]) for i, (a, b) in enumerate(pieces)])
    copies[0].wait()
    pick = picks(halo_ref[...], me_ref[0], tokens, True)
    for i in (0, 1):
        copies[1 + i].wait()
        rows = dot(pick, pack_ref[:, (2 + i) * width : (3 + i) * width])
        send_ref[:, :, i * width : (i + 1) * width] = rows.reshape(domains, cap, width).astype(BF)
    outs = start([(send_ref, send_hbm, sems.at[len(pieces)])])
    for copy in copies[3:]:
        copy.wait()
    product = pack_ref[:, width : 2 * width].astype(F32) * saved_ref[...].astype(F32)
    high = product.astype(BF)
    low = (product - high.astype(F32)).astype(BF)
    member = one_where(iota((heads, width), 1) // head_dim == iota((heads, width), 0))
    delta = dot_nt(member, high) + dot_nt(member, low)
    parts = [p.astype(F32) for p in split3(logsum_ref[...]) + split3(delta)]
    parts.append(jnp.zeros((LANES - 6 * heads, tokens), F32))
    extra_ref[...] = jnp.concatenate(parts, axis=0).T.astype(BF)
    pack_ref[:, 4 * width :] = extra_ref[...]
    for copy in outs:
        copy.wait()


def extra_mask(head, heads, first):
    lane = iota((16, LANES), 1)
    inside = (lane >= first) & (lane < first + 3 * heads)
    return one_where(inside & (lane % heads == head))


def rows_of(pattern, tokens):
    return jnp.concatenate([pattern] * (tokens // pattern.shape[0]), axis=0)


def half_masks(tokens, head_dim):
    low = one_where(iota((16, LANES), 1) < head_dim)
    high = one_where(iota((16, LANES), 1) >= head_dim)
    return rows_of(low, tokens), rows_of(high, tokens)


def pair_dots(rows, row_extra, columns):
    return tuple(
        dot_nt(jnp.concatenate([row, extra], axis=1), column)
        for row, extra, column in zip(rows, row_extra, columns, strict=True)
    )


def pair_weights(dots, scale):
    score, grad = dots
    weight = jnp.exp2(score * (scale * math.log2(math.e)))
    return weight.astype(BF), (weight * grad).astype(BF)


def staged(count, first, second):
    ahead = first(0)
    for pair in range(count):
        now, ahead = ahead, first(pair + 1) if pair + 1 < count else None
        second(pair, now)


def minus_constants(rows, scale):
    return jnp.full((rows, LANES), -1.0 / scale, BF), jnp.full((rows, LANES), -1.0, BF)


def asking(query, cot, extra, pair, heads, masks):
    two_query, two_cot = two_heads(query, masks), two_heads(cot, masks)
    columns = (
        jnp.concatenate([two_query, two_extras(extra, pair, heads, 0)], axis=1),
        jnp.concatenate([two_cot, two_extras(extra, pair, heads, 3 * heads)], axis=1),
    )
    return two_query, two_cot, columns


def diagonal(product, tokens, head_dim):
    return jnp.concatenate([product[:head_dim, :tokens], product[head_dim:, tokens:]], axis=0)


def two_heads(block, masks):
    return jnp.concatenate([block * masks[0], block * masks[1]], axis=0)


def two_extras(extra, pair, heads, first):
    tokens = extra.shape[0]
    return jnp.concatenate(
        [extra * rows_of(extra_mask(2 * pair + i, heads, first), tokens) for i in (0, 1)], axis=0
    )


def halo_kernel(
    heads,
    block_ref,
    pack_ref,
    recv_ref,
    part_hbm,
    low_hbm,
    pool_hbm,
    back_hbm,
    pool,
    part,
    low,
    back,
    sems,
):
    tokens = pack_ref.shape[0]
    domains, cap, wide = recv_ref.shape
    width = wide // 2
    head_dim = width // heads
    scale = head_dim**-0.5
    local = block_ref[0] == 0

    @pl.when(local)
    def _():
        pool[:tokens] = pack_ref[:, 2 * width : 3 * width]
        pool[tokens:] = pack_ref[:, 3 * width : 4 * width]

    @pl.when(jnp.logical_not(local))
    def _():
        for i in (0, 1):
            rows = recv_ref[:, :, i * width : (i + 1) * width].astype(F32)
            pool[i * tokens : (i + 1) * tokens] = rows.reshape(domains * cap, width).astype(BF)

    outs = start([(pool.at[:tokens], pool_hbm, sems.at[0])])
    masks = half_masks(tokens, head_dim)
    constants = minus_constants(tokens, scale)
    to_own = jnp.where(local, 1.0, 0.0)
    to_halo = 1.0 - to_own

    def first(pair):
        at = pair * LANES
        query, cot = pack_ref[:, at : at + LANES], pack_ref[:, width + at : width + at + LANES]
        two_query, two_cot, columns = asking(
            query, cot, pack_ref[:, 4 * width :], pair, heads, masks
        )
        rows = pool[:tokens, at : at + LANES], pool[tokens:, at : at + LANES]
        return two_query, two_cot, pair_dots(rows, constants, columns)

    def second(pair, stage):
        at = pair * LANES
        two_query, two_cot, dots = stage
        weight_low, grad_low = pair_weights(dots, scale)
        low[:, 2 * at : 2 * at + 2 * LANES] = grad_low
        key_grad = dot(grad_low, two_query) * scale
        value_grad = dot(weight_low, two_cot)
        part[:tokens, at : at + LANES] = key_grad * to_own
        part[tokens:, at : at + LANES] = value_grad * to_own
        for i, grad in enumerate((key_grad, value_grad)):
            rows = (grad * to_halo).reshape(domains, cap, LANES)
            back[:, :, i * width + at : i * width + at + LANES] = rows.astype(BF)
        if pair % 4 != 3:
            return
        lanes = slice(at - 3 * LANES, at + LANES)
        wide = slice(2 * (at - 3 * LANES), 2 * (at + LANES))
        beside = slice(width + at - 3 * LANES, width + at + LANES)
        index = 4 * (pair // 4)
        outs.extend(
            start(
                [
                    (back.at[:, :, lanes], back_hbm.at[:, :, lanes], sems.at[index + 1]),
                    (back.at[:, :, beside], back_hbm.at[:, :, beside], sems.at[index + 2]),
                    (part.at[:, lanes], part_hbm.at[:, lanes], sems.at[index + 3]),
                    (low.at[:, wide], low_hbm.at[:, wide], sems.at[index + 4]),
                ]
            )
        )

    staged(heads // 2, first, second)
    for copy in outs:
        copy.wait()


def own_keys(keys, values, pair, heads, masks, scale):
    tokens = keys.shape[0]
    return tuple(
        jnp.concatenate(
            [
                two_heads(block, masks),
                jnp.concatenate(
                    [rows_of(extra_mask(2 * pair + i, heads, at) * BF(by), tokens) for i in (0, 1)],
                    axis=0,
                ),
            ],
            axis=1,
        )
        for block, at, by in ((keys, 0, -1.0 / scale), (values, 3 * heads, -1.0))
    )


def both_sides(heads, width, pack_ref, other, ready, before, finish):
    tokens = pack_ref.shape[0]
    head_dim = width // heads
    scale = head_dim**-0.5
    masks = half_masks(tokens, head_dim)
    constants = minus_constants(tokens, scale)

    def blocks(ref, pair):
        starts = [i * width + pair * LANES for i in range(4)]
        return [ref[:, at : at + LANES] for at in starts]

    def first(pair):
        ready(pair)
        query, cot, key, value = blocks(pack_ref, pair)
        their_query, their_cot, their_key, their_value = blocks(other, pair)
        extra = other[:, 4 * width :]
        _, _, columns = asking(query, cot, pack_ref[:, 4 * width :], pair, heads, masks)
        under = pair_dots(
            (their_query, their_cot), (extra, extra), own_keys(key, value, pair, heads, masks, scale)
        )
        over = pair_dots((their_key, their_value), constants, columns)
        return under, over

    def second(pair, stage):
        under, over = stage
        their_query, their_cot, their_key, _ = blocks(other, pair)
        weight_low, grad_low = pair_weights(under, scale)
        _, query_low = pair_weights(over, scale)
        keys, lows = before(pair, their_key, query_low)
        query_grad = diagonal(dot_tn(keys, lows), tokens, head_dim)
        key_grad = diagonal(dot_tn(their_query, grad_low), tokens, head_dim)
        value_grad = diagonal(dot_tn(their_cot, weight_low), tokens, head_dim)
        finish(pair, (query_grad * scale).T, (key_grad * scale).T, value_grad.T)

    staged(heads // 2, first, second)


def early_kernel(
    heads,
    me_ref,
    halo_hbm,
    pack_ref,
    other_hbm,
    low_hbm,
    pool_hbm,
    part_hbm,
    grads_hbm,
    place_ref,
    halo_ref,
    other,
    low,
    pool,
    part,
    grads,
    sems,
):
    tokens, width = pool_hbm.shape
    copies = start(
        [
            (other_hbm, other, sems.at[0]),
            (low_hbm, low, sems.at[1]),
            (pool_hbm, pool, sems.at[2]),
            (part_hbm, part, sems.at[3]),
            (halo_hbm, halo_ref, sems.at[4]),
        ]
    )
    copies[4].wait()
    place_ref[...] = picks(halo_ref[...], me_ref[0], tokens, False)
    copies[0].wait()
    outs = []

    def ready(pair):
        pass

    def before(pair, keys, query_low):
        if pair == 0:
            for copy in copies[1:4]:
                copy.wait()
        at = pair * LANES
        listed = low[:, 2 * at : 2 * at + 2 * LANES]
        return (
            jnp.concatenate([keys, pool[:, at : at + LANES]], axis=0),
            jnp.concatenate([query_low, listed], axis=0),
        )

    def finish(pair, query_grad, key_grad, value_grad):
        lanes = slice(pair * LANES, (pair + 1) * LANES)
        grads[:tokens, lanes] = query_grad
        grads[tokens : 2 * tokens, lanes] = part[:tokens, lanes] + key_grad
        grads[2 * tokens :, lanes] = part[tokens:, lanes] + value_grad
        if pair % 4 == 3:
            done = slice((pair - 3) * LANES, (pair + 1) * LANES)
            outs.extend(
                start([(grads.at[:, done], grads_hbm.at[:, done], sems.at[5 + pair // 4])])
            )

    both_sides(heads, width, pack_ref, other, ready, before, finish)
    for copy in outs:
        copy.wait()


def late_kernel(
    heads,
    own_query_hbm,
    own_cot_hbm,
    own_key_hbm,
    own_value_hbm,
    extra_ref,
    other_hbm,
    grads_hbm,
    place_ref,
    returned_ref,
    query_hbm,
    key_hbm,
    value_hbm,
    own,
    other,
    grads,
    result,
    sems,
):
    tokens, width = query_hbm.shape
    domains, cap, _ = returned_ref.shape
    half = width // 2

    def load(side):
        owned = (own_query_hbm, own_cot_hbm, own_key_hbm, own_value_hbm)
        part = slice(side * half, (side + 1) * half)
        blocks = [slice(i * width + side * half, i * width + (side + 1) * half) for i in range(4)]
        at = 9 * side
        triples = [
            (other_hbm.at[:, block], other.at[:, block], sems.at[at + i])
            for i, block in enumerate(blocks)
        ]
        triples += [
            (hbm.at[:, part], own.at[:, block], sems.at[at + 4 + i])
            for i, (hbm, block) in enumerate(zip(owned, blocks, strict=True))
        ]
        triples.append((grads_hbm.at[:, part], grads.at[:, part], sems.at[at + 8]))
        return start(triples)

    beside = slice(4 * width, 4 * width + LANES)
    extra = start([(other_hbm.at[:, beside], other.at[:, beside], sems.at[18])])
    copies = load(0), load(1)
    own[:, 4 * width :] = extra_ref[...]
    outs = []

    def ready(pair):
        if pair == 0:
            for copy in extra + copies[0][:8]:
                copy.wait()
        if pair == heads // 4:
            for copy in copies[1][:8]:
                copy.wait()

    def before(pair, keys, query_low):
        if pair == 0:
            copies[0][8].wait()
            copies[1][8].wait()
        return keys, query_low

    def returned_rows(pair, i):
        at = i * width + pair * LANES
        rows = returned_ref[:, :, at : at + LANES].astype(F32)
        return dot(place_ref[...], rows.reshape(domains * cap, LANES).astype(BF))

    def finish(pair, query_grad, key_grad, value_grad):
        lanes = slice(pair * LANES, (pair + 1) * LANES)
        ends = query_grad, key_grad + returned_rows(pair, 0), value_grad + returned_rows(pair, 1)
        rows = [slice(i * tokens, (i + 1) * tokens) for i in range(3)]
        for row, end in zip(rows, ends, strict=True):
            result[row, lanes] = (grads[row, lanes] + end).astype(BF)
        if pair % 4 == 3:
            done = slice((pair - 3) * LANES, (pair + 1) * LANES)
            outs.extend(
                start(
                    [
                        (result.at[row, done], hbm.at[:, done], sems.at[19 + 3 * (pair // 4) + i])
                        for i, (row, hbm) in enumerate(
                            zip(rows, (query_hbm, key_hbm, value_hbm), strict=True)
                        )
                    ]
                )
            )

    both_sides(heads, width, own, other, ready, before, finish)
    for copy in outs:
        copy.wait()


SMEM, VMEM, HBM = pltpu.SMEM, pltpu.VMEM, pltpu.HBM


def call(kernel, ins, outs, cost, scratch, sems):
    run = pl.pallas_call(
        kernel,
        out_shape=tuple(space(shape, kind) for shape, kind, space in outs),
        in_specs=[pl.BlockSpec(memory_space=space) for space in ins],
        out_specs=tuple(pl.BlockSpec(memory_space=space) for _, _, space in outs),
        scratch_shapes=[pltpu.VMEM(*s) for s in scratch] + [pltpu.SemaphoreType.DMA((sems,))],
        compiler_params=pltpu.CompilerParams(vmem_limit_bytes=VMEM_LIMIT),
        cost_estimate=pl.CostEstimate(flops=cost[0], bytes_accessed=cost[1], transcendentals=0),
    )

    def placed(*args):
        return run(
            *(
                pltpu.with_memory_space_constraint(x, space) if space is HBM else x
                for x, space in zip(args, ins, strict=True)
            )
        )

    return placed


def swap(block, axis, first):
    size = lax.axis_size(axis)
    pairs = [(i, i + 1) for i in range(first, size - 1, 2)]
    return lax.ppermute(block, axis, pairs + [(b, a) for a, b in pairs])


def backward(
    query_matrix,
    key_matrix,
    value_matrix,
    saved_output,
    output_grad,
    row_logsum,
    key_blocks,
    halo_rows,
):
    queries, keys, values = query_matrix[0], key_matrix[0], value_matrix[0]
    saved, cotangent, logsum = saved_output[0], output_grad[0], row_logsum[0]
    tokens, width = queries.shape
    heads = logsum.shape[0]
    domains, _, cap = halo_rows.shape
    slots = domains * cap
    me = lax.axis_index("dom").astype(jnp.int32).reshape(1)
    halo = halo_rows.transpose(0, 2, 1)
    array = tokens * width
    packed = 4 * width + LANES

    def exchange(block):
        return lax.all_to_all(block, "dom", split_axis=0, concat_axis=0, tiled=True)

    pack, extra, send = call(
        front_kernel,
        (SMEM,) + (HBM,) * 7,
        (
            ((tokens, packed), BF, VMEM),
            ((tokens, LANES), BF, VMEM),
            ((domains, cap, 2 * width), BF, HBM),
        ),
        (2 * slots * array, 20 * array),
        (
            (halo.shape, jnp.int32),
            ((tokens, width), BF),
            (logsum.shape, F32),
            ((domains, cap, 2 * width), BF),
        ),
        8,
    )(me, halo, queries, keys, values, cotangent, saved, logsum)
    received = exchange(send)
    odd = swap(pack, "hour", 1)
    even = swap(pack, "hour", 0)
    part, low, pool, back = call(
        functools.partial(halo_kernel, heads),
        (SMEM, VMEM, VMEM),
        (
            ((2 * tokens, width), F32, HBM),
            ((tokens, 2 * width), BF, HBM),
            ((tokens, width), BF, HBM),
            ((domains, cap, 2 * width), BF, HBM),
        ),
        (20 * tokens * array, 30 * array),
        (
            ((2 * tokens, width), BF),
            ((2 * tokens, width), F32),
            ((tokens, 2 * width), BF),
            ((domains, cap, 2 * width), BF),
        ),
        1 + heads // 2,
    )(key_blocks.reshape(1), pack, received)
    returned = exchange(back)
    grads, place = call(
        functools.partial(early_kernel, heads),
        (SMEM, HBM, VMEM, pl.ANY, HBM, HBM, HBM),
        (((3 * tokens, width), F32, HBM), ((tokens, slots), BF, VMEM)),
        (30 * tokens * array, 40 * array),
        (
            (halo.shape, jnp.int32),
            ((tokens, packed), BF),
            ((tokens, 2 * width), BF),
            ((tokens, width), BF),
            ((2 * tokens, width), F32),
            ((3 * tokens, width), F32),
        ),
        5 + heads // 8,
    )(me, halo, pack, even, low, pool, part)
    query_grad, key_grad, value_grad = call(
        functools.partial(late_kernel, heads),
        (HBM, HBM, HBM, HBM, VMEM, pl.ANY, HBM, VMEM, VMEM),
        (((tokens, width), BF, HBM),) * 3,
        (30 * tokens * array, 40 * array),
        (
            ((tokens, packed), BF),
            ((tokens, packed), BF),
            ((3 * tokens, width), F32),
            ((3 * tokens, width), BF),
        ),
        19 + 3 * (heads // 8),
    )(queries, cotangent, keys, values, extra, odd, grads, place, returned)
    return query_grad[None], key_grad[None], value_grad[None]


def solution(mesh):
    in_specs = (
        P("hour", "dom", None),
        P("hour", "dom", None),
        P("hour", "dom", None),
        P("hour", "dom", None),
        P("hour", "dom", None),
        P("hour", None, "dom"),
        P("dom", None),
        P(),
    )
    out_specs = (P("hour", "dom", None), P("hour", "dom", None), P("hour", "dom", None))
    return jax.shard_map(
        backward, mesh=mesh, in_specs=in_specs, out_specs=out_specs, check_vma=False
    )
```
